512 devices in a mesh: hyp: 8 (over y), prow: 16 (over x, z_lo), pcol: 4 (over z_hi, core).
Axes of the slice: x: 4, y: 8, z: 8 (z_hi: 2, z_lo: 4; z = z_hi * 4 + z_lo), core: 2. Of those that a mesh axis runs over, the one named last changes fastest.
Arguments:
- sigma_rows: bfloat16 [8, 8192, 8192], P('hyp', 'prow', 'pcol'), may hold values from -1 to 1, as said below
- panel: bfloat16 [8, 8192, 2, 384], P('hyp', ('prow', 'pcol')), may hold values from -0.59765625 to 0.59765625
- live_block_rows: int32 [2, 64], P(None, ('prow', 'pcol')), may hold values from 1 to 128, 6144 in all within a row
- inv_diag: bfloat16 [8, 2, 384, 384], P('hyp', None, ('prow', 'pcol')), may hold values from -0.3125 to 0.3125
- quad_weight: float32 [8], P('hyp'), may hold values from 0.05 to 0.5
Outputs:
- sigma_panel: bfloat16 [8, 8192, 2, 384], P('hyp', ('prow', 'pcol'))
- marginal: float32 [2, 384, 384], replicated
The draws below stay inside these ranges and needn't reach their ends.
Inputs may be any that keep to these rules, and one draw needn't show every extreme that they name: `sigma_rows`: each quadrature point's matrix is symmetric.
All inputs are finite; a program needn't handle non-finite values. No bound on the sum of `live_block_rows` on one device may be relied on, other than what follows from the above.
Results may differ from the reference program's by a relative error of at most 0.0004.
Values may be sent and summed in bfloat16 or wider, within the bound.
A program may use at most 64 MiB of HBM per device.

```python
import math
import jax
import jax.numpy as jnp
import numpy as np
from jax import lax

W = 384
NS = 2
BLOCK = 128
NB = 64
R = 8192
HYP = 8


def draw_sigma_rows(key, part):
    pairing = jax.random.permutation(jax.random.fold_in(key, 7), NB)
    blocks = jnp.arange(R, dtype=jnp.int32) // BLOCK
    spike = 1.0 + 3.0 * (pairing[blocks][:, None] == blocks[None, :]).astype(jnp.float32)
    spread = math.sqrt(2.0) * (R // 4) ** (-0.5)

    def one_point(point_key):
        values = jax.random.normal(point_key, (R, R), jnp.float32)
        values = values * spread * spike
        values = 0.5 * (values + values.T)
        return jnp.clip(values, -1.0, 1.0).astype(jnp.bfloat16)
    point_keys = jax.random.split(jax.random.fold_in(key, 11), HYP)
    return lax.map(one_point, point_keys)


def block_scale(rng, shape, cuts, smallest, high):
    def one(axis_at, parts):
        steps = jax.random.uniform(jax.random.fold_in(jax.random.fold_in(rng, 6), axis_at), (parts,), jnp.float32, smallest / len(cuts), high / len(cuts))
        return jnp.repeat(jnp.exp(steps), shape[axis_at] // parts).reshape((-1,) + (1,) * (len(shape) - axis_at - 1))

    factor_of = one(*cuts[0])
    for cut in cuts[1:]:
        factor_of = factor_of * one(*cut)
    return factor_of


def split_up(count, total, most, lean):
    loads = [(1 << 20) // math.isqrt(grade ** lean) + 1 for grade in range(2, count + 1)]
    rest, given = total - most - (count - 1), [1] * (count - 1)
    while rest > 0:
        free = [i for i in range(count - 1) if given[i] < most]
        mass, remaining = sum([loads[i] for i in free]), rest
        for i in free:
            more = min(most - given[i], max(1, remaining * loads[i] // mass), rest)
            given[i] = given[i] + more
            rest = rest - more
    return np.array([most] + given)


def ragged(key, count, total, limit, skew):
    if count == 2:
        one = jax.random.randint(key, (), max(1, total - limit), min(limit, total - 1) + 1)
        return jnp.stack([one, total - one])
    tallies = jnp.asarray(split_up(count, total, limit, skew), jnp.int32)
    pairs = (count - 1) // 2
    giver, taker = tallies[1:1 + 2 * pairs:2], tallies[2:2 + 2 * pairs:2]
    room = jnp.minimum(giver - 1, limit - taker)
    passed = jax.random.randint(jax.random.fold_in(key, 1), (pairs,), 0, 1 << 20) % (room + 1)
    tallies = tallies.at[1:1 + 2 * pairs:2].set(giver - passed).at[2:2 + 2 * pairs:2].set(taker + passed)
    return tallies[jax.random.permutation(jax.random.fold_in(key, 2), count)]


def normal_values(key, extent, scale, limit, cuts=(), kind=jnp.bfloat16):
    entries = jax.random.normal(key, extent, jnp.float32) * scale
    if len(cuts) > 0:
        entries = block_scale(key, extent, cuts, -0.22, 0.18) * entries
    return jnp.clip(entries, min=-limit, max=limit).astype(kind)


def setup_inputs(seed: int = 0) -> dict:
    streams_of = jax.random.split(jax.random.key(seed), 6)
    sigma_rows = draw_sigma_rows(jax.random.fold_in(streams_of[5], 71), 0)
    panel = normal_values(streams_of[1], (HYP, R, NS, W), 0.1, 0.59765625, ((0, 8), (1, 64)))
    live_block_rows = jax.vmap(lambda own: ragged(own, NB, NB * BLOCK * 3 // 4, BLOCK, 2))(jax.random.split(streams_of[2], NS)).reshape((NS, NB)).astype(jnp.int32)
    inv_diag = normal_values(streams_of[3], (HYP, NS, W, W), W ** -0.5, 0.3125, ((0, 8), (2, 64)))
    quad_weight = jnp.clip(jnp.exp(math.log(0.5) - 2.3025851 * jax.random.uniform(streams_of[4], (HYP,), jnp.float32) ** block_scale(streams_of[4], (HYP,), ((0, 8),), -0.2, 0.2)), 0.05, 0.5)
    return {"sigma_rows": sigma_rows, "panel": panel, "live_block_rows": live_block_rows, "inv_diag": inv_diag, "quad_weight": quad_weight}


def reference(sigma_rows, panel, live_block_rows, inv_diag, quad_weight):
    offsets = jnp.arange(R, dtype=jnp.int32) % BLOCK
    block_index = jnp.arange(R, dtype=jnp.int32) // BLOCK
    active = (offsets[None, :] < live_block_rows[:, block_index]).T
    masked_panel = jnp.where(active[None, :, :, None], panel, jnp.zeros_like(panel)).astype(jnp.bfloat16)

    def one_group(operands):
        covariance_block, single_masked_panel, inverse = operands
        applied = jnp.dot(covariance_block, single_masked_panel.reshape(R, NS * W), preferred_element_type=jnp.float32)
        applied_full = applied.reshape(R, NS, W)
        half_applied_product = applied_full.astype(jnp.bfloat16)
        panel_out = jnp.where(active[:, :, None], -half_applied_product, jnp.zeros_like(half_applied_product))
        coupling_block = jnp.einsum("vwg,vwe->wge", single_masked_panel.astype(jnp.float32), applied_full, precision=lax.Precision.HIGHEST)
        diagonal = jnp.einsum("skp,skq->spq", inverse.astype(jnp.float32), inverse.astype(jnp.float32), precision=lax.Precision.HIGHEST)
        return panel_out, coupling_block + diagonal

    sigma_panel, diagonal = lax.map(one_group, (sigma_rows, masked_panel, inv_diag))
    marginal = jnp.einsum("h,hspq->spq", quad_weight, diagonal, precision=lax.Precision.HIGHEST)
    return sigma_panel, marginal
```

```python
import functools

import jax
import jax.numpy as jnp
from jax import lax
from jax.experimental import pallas as pl
from jax.experimental.pallas import tpu as pltpu
from jax.sharding import PartitionSpec as P

MESH = pl.DeviceIdType.MESH
NX, NZ, NY = 4, 8, 8
CHUNKS = 3
T = 128


def place(y, x, z, k):
    return (y, x * 4 + z % 4, (z // 4) * 2 + k)


def remote(src, dst, send, recv, device):
    return pltpu.make_async_remote_copy(
        src_ref=src, dst_ref=dst, send_sem=send, recv_sem=recv, device_id=device, device_id_type=MESH
    )


def arrived(ref, sem):
    pltpu.make_async_copy(ref, ref, sem).wait()


def pairs():
    return [(s, i, j) for s in range(2) for j in range(3) for i in range(j + 1)]


def kernel(
    w, m, inv, sig, out, marg,
    sg, q, f, wp, pr, sb, zb, d, dr, e, xr, e2, zr, yr, g,
    ssig, sloc, s1, r1, s2, r2, s3, r3, s4, r4, s5, r5, s6, r6,
    sa, ra, sx, rx, sz, rz, sy, ry, sgz, rgz, sgx, rgx, sc, rc,
):
    cw = 768 // CHUNKS
    sub = cw // T
    y = lax.axis_index("hyp")
    prow = lax.axis_index("prow")
    pcol = lax.axis_index("pcol")
    x, zl = prow // 4, prow % 4
    zh, k = pcol // 2, pcol % 2
    z = zh * 4 + zl
    slot = zl * 4 + zh * 2
    right, left = (x + 1) % NX, (x + 3) % NX

    barrier = pltpu.get_barrier_semaphore()
    greet = [place(y, x, z, 1 - k)]
    greet += [place(y, (x + a) % NX, z, c) for a in range(1, NX) for c in range(2)]
    greet += [place(y, x, (z + a) % NZ, k) for a in range(1, NZ)]
    greet += [place((y + a) % NY, x, z, k) for a in range(1, NY)]
    for who in greet:
        pl.semaphore_signal(barrier, inc=1, device_id=who, device_id_type=MESH)
    sigma_copy = pltpu.make_async_copy(sig, sg, ssig)
    sigma_copy.start()
    pl.semaphore_wait(barrier, len(greet))

    sends = []

    def go(copy):
        copy.start()
        sends.append(copy)

    kd = x % 2
    half = x // 2
    for ch in range(CHUNKS):
        own = m.at[ch, pl.ds(pl.multiple_of(x * 32, 32), 32)]

        @pl.when(kd == k)
        def _():
            local = pltpu.make_async_copy(own, q.at[ch, half, k], r1.at[ch])
            local.start()

        @pl.when(kd != k)
        def _():
            copy = remote(own, q.at[ch, half, k], s1.at[ch, 0], r1.at[ch], place(y, x, z, 1 - k))
            copy.start()

        for a in range(1, NX):
            xt = (x + a) % NX
            rows = m.at[ch, pl.ds(pl.multiple_of(xt * 32, 32), 32)]
            go(remote(rows, q.at[ch, half, k], s1.at[ch, a], r1.at[ch], place(y, xt, z, kd)))

    weight = w[...]
    for t, (s, i, j) in enumerate(pairs()):
        d[t] = weight * lax.dot_general(
            inv[s, :, i * T:(i + 1) * T], inv[s, :, j * T:(j + 1) * T],
            (((0,), (0,)), ((), ())), preferred_element_type=jnp.float32,
        )

    for ch in range(CHUNKS):
        arrived(q.at[ch], r1.at[ch])
        for n, a in enumerate((4, 3, 5, 2, 6, 1, 7)):
            zt = (z + a) % NZ
            go(remote(
                q.at[ch, zt // 4], f.at[ch, pl.ds(slot, 2), x], s2.at[ch, n], r2.at[ch], place(y, x, zt, k)
            ))
        pltpu.make_async_copy(q.at[ch, zh], f.at[ch, pl.ds(slot, 2), x], r2.at[ch]).start()

    to_right, to_left = place(y, right, z, k), place(y, left, z, k)

    def ring_own(ch):
        arrived(f.at[ch, :, x], r2.at[ch])
        lo, hi = f.at[ch, 0:8, x], f.at[ch, 8:16, x]
        go(remote(lo, lo, s3.at[ch, 0], r3.at[ch, 0], to_right))
        go(remote(hi, hi, s3.at[ch, 1], r3.at[ch, 1], to_left))
        go(remote(hi, hi, s3.at[ch, 2], r3.at[ch, 2], to_right))
        go(remote(lo, lo, s3.at[ch, 3], r3.at[ch, 3], to_left))

    def ring_relay(ch):
        lo, hi = f.at[ch, 0:8, left], f.at[ch, 8:16, right]
        arrived(lo, r3.at[ch, 0])
        go(remote(lo, lo, s4.at[ch, 0], r4.at[ch, 0], to_right))
        arrived(hi, r3.at[ch, 1])
        go(remote(hi, hi, s4.at[ch, 1], r4.at[ch, 1], to_left))

    def multiply(ch):
        far = (x + 2) % NX
        arrived(f.at[ch, 8:16, left], r3.at[ch, 2])
        arrived(f.at[ch, 0:8, right], r3.at[ch, 3])
        arrived(f.at[ch, 0:8, far], r4.at[ch, 0])
        arrived(f.at[ch, 8:16, far], r4.at[ch, 1])
        product = jnp.dot(sg[...], f[ch].reshape(2048, cw), preferred_element_type=jnp.float32)
        wp[ch] = product.reshape(2, 2, T, cw)
        go(remote(wp.at[ch, :, 1 - k], pr.at[ch], s5.at[ch], r5.at[ch], place(y, x, z, 1 - k)))

    def cross(ch):
        arrived(pr.at[ch], r5.at[ch])
        sb[ch] = wp[ch, 1 - zh, k] + pr[ch, 1 - zh]
        go(remote(sb.at[ch], zb.at[ch], s6.at[ch], r6.at[ch], place(y, x, (z + 4) % NZ, k)))

    def finish(ch):
        arrived(zb.at[ch], r6.at[ch])
        applied = (wp[ch, zh, k] + pr[ch, zh]) + zb[ch]
        high = applied.astype(jnp.bfloat16)
        out[ch] = -high
        low = (applied - high.astype(jnp.float32)).astype(jnp.bfloat16)
        for b in range(sub):
            s, j = divmod(ch * sub + b, 3)
            for i in range(j + 1):
                c0, b0 = divmod(s * 3 + i, sub)
                mine = m[c0, :, b0 * T:(b0 + 1) * T]
                dims = (((0,), (0,)), ((), ()))
                tile = lax.dot_general(
                    mine, high[:, b * T:(b + 1) * T], dims, preferred_element_type=jnp.float32
                ) + lax.dot_general(
                    mine, low[:, b * T:(b + 1) * T], dims, preferred_element_type=jnp.float32
                )
                at = pairs().index((s, i, j))
                d[at] = d[at] + weight * tile

    for t in range(CHUNKS + 4):
        if t < CHUNKS:
            ring_own(t)
        if 0 <= t - 1 < CHUNKS:
            ring_relay(t - 1)
        if t == 2:
            sigma_copy.wait()
        if 0 <= t - 2 < CHUNKS:
            multiply(t - 2)
        if 0 <= t - 3 < CHUNKS:
            cross(t - 3)
        if 0 <= t - 4 < CHUNKS:
            finish(t - 4)

    go(remote(d.at[pl.ds((1 - k) * 6, 6)], dr, sa, ra, place(y, x, z, 1 - k)))
    arrived(dr, ra)
    e[...] = (d[pl.ds(k * 6, 6)] + dr[...]).reshape(NX, 192, T)
    for a in range(1, NX):
        xt = (x + a) % NX
        go(remote(e.at[xt], xr.at[a - 1], sx.at[a - 1], rx, place(y, xt, z, k)))
    arrived(xr, rx)
    e2[...] = (((e[x] + xr[0]) + xr[1]) + xr[2]).reshape(NZ, 24, T)
    for a in range(1, NZ):
        zt = (z + a) % NZ
        go(remote(e2.at[zt], zr.at[a - 1], sz.at[a - 1], rz, place(y, x, zt, k)))
    arrived(zr, rz)
    total = e2[z]
    for a in range(NZ - 1):
        total = total + zr[a]
    yr[y] = total
    for a in range(1, NY):
        go(remote(yr.at[y], yr.at[y], sy.at[a - 1], ry, place((y + a) % NY, x, z, k)))
    arrived(yr.at[0:7], ry)
    total = yr[0]
    for a in range(1, NY):
        total = total + yr[a]
    g[k, x, z] = total
    for a in range(1, NZ):
        go(remote(g.at[k, x, z], g.at[k, x, z], sgz.at[a - 1], rgz, place(y, x, (z + a) % NZ, k)))
    arrived(g.at[0, 0, 0:7], rgz)
    for a in range(1, NX):
        go(remote(g.at[k, x], g.at[k, x], sgx.at[a - 1], rgx, place(y, (x + a) % NX, z, k)))
    arrived(g.at[0, 0:3], rgx)
    go(remote(g.at[k], g.at[k], sc, rc, place(y, x, z, 1 - k)))
    arrived(g.at[0], rc)
    for s in range(2):
        whole = g[s].reshape(6, T, T)
        for t, (u, i, j) in enumerate(pairs()[:6]):
            marg[s, i * T:(i + 1) * T, j * T:(j + 1) * T] = whole[t]
            if i != j:
                marg[s, j * T:(j + 1) * T, i * T:(i + 1) * T] = whole[t].T

    for copy in sends:
        copy.wait_send()
    for ch in range(CHUNKS):
        own = m.at[ch, pl.ds(pl.multiple_of(x * 32, 32), 32)]

        @pl.when(kd != k)
        def _():
            remote(own, q.at[ch, half, k], s1.at[ch, 0], r1.at[ch], place(y, x, z, 1 - k)).wait_send()


def on_device(sigma_rows, panel, live_block_rows, inv_diag, quad_weight):
    cw = 768 // CHUNKS
    offsets = lax.broadcasted_iota(jnp.int32, (128, 2, 384), 0)
    active = offsets < live_block_rows[:, 0][None, :, None]
    masked = jnp.where(active, panel[0], jnp.zeros_like(panel[0])).reshape(128, CHUNKS, cw)
    masked = jnp.transpose(masked, (1, 0, 2))
    inv = jnp.pad(inv_diag[0], ((0, 0), (0, 10), (0, 0)))
    weight = jnp.broadcast_to(quad_weight[:, None], (1, 128))
    f32, bf16 = jnp.float32, jnp.bfloat16
    dma = pltpu.SemaphoreType.DMA
    vmem = pl.BlockSpec(memory_space=pltpu.VMEM)
    negated, marginal = pl.pallas_call(
        kernel,
        out_shape=(
            jax.ShapeDtypeStruct((CHUNKS, 128, cw), bf16),
            jax.ShapeDtypeStruct((2, 384, 384), f32),
        ),
        in_specs=[vmem, vmem, vmem, pl.BlockSpec(memory_space=pl.ANY)],
        out_specs=(vmem, vmem),
        scratch_shapes=[
            pltpu.VMEM((512, 2048), bf16),
            pltpu.VMEM((CHUNKS, 2, 2, 32, cw), bf16),
            pltpu.VMEM((CHUNKS, 16, 4, 32, cw), bf16),
            pltpu.VMEM((CHUNKS, 2, 2, T, cw), f32),
            pltpu.VMEM((CHUNKS, 2, T, cw), f32),
            pltpu.VMEM((CHUNKS, T, cw), f32),
            pltpu.VMEM((CHUNKS, T, cw), f32),
            pltpu.VMEM((12, T, T), f32),
            pltpu.VMEM((6, T, T), f32),
            pltpu.VMEM((NX, 192, T), f32),
            pltpu.VMEM((NX - 1, 192, T), f32),
            pltpu.VMEM((NZ, 24, T), f32),
            pltpu.VMEM((NZ - 1, 24, T), f32),
            pltpu.VMEM((NY, 24, T), f32),
            pltpu.VMEM((2, NX, NZ, 24, T), f32),
            dma, dma,
            dma((CHUNKS, 4)), dma((CHUNKS,)),
            dma((CHUNKS, 7)), dma((CHUNKS,)),
            dma((CHUNKS, 4)), dma((CHUNKS, 4)),
            dma((CHUNKS, 2)), dma((CHUNKS, 2)),
            dma((CHUNKS,)), dma((CHUNKS,)),
            dma((CHUNKS,)), dma((CHUNKS,)),
            dma, dma,
            dma((3,)), dma,
            dma((7,)), dma,
            dma((7,)), dma,
            dma((7,)), dma,
            dma((3,)), dma,
            dma, dma,
        ],
        compiler_params=pltpu.CompilerParams(
            collective_id=0, has_side_effects=True, vmem_limit_bytes=56 * 1024 * 1024
        ),
    )(weight, masked, inv, sigma_rows[0])
    applied = jnp.transpose(negated, (1, 0, 2)).reshape(128, 2, 384)
    sigma_panel = jnp.where(active, applied, jnp.zeros_like(applied))[None]
    return (sigma_panel, marginal)


def solution(mesh):
    in_specs = (
        P("hyp", "prow", "pcol"),
        P("hyp", ("prow", "pcol"), None, None),
        P(None, ("prow", "pcol")),
        P("hyp", None, ("prow", "pcol"), None),
        P("hyp"),
    )
    out_specs = (P("hyp", ("prow", "pcol"), None, None), P())
    return jax.shard_map(
        on_device, mesh=mesh, in_specs=in_specs, out_specs=out_specs, check_vma=False
    )
```

```python
import jax
import jax.numpy as jnp
from jax import lax
from jax.experimental import pallas as pl
from jax.experimental.pallas import tpu as pltpu
from jax.sharding import PartitionSpec as P

MESH = pl.DeviceIdType.MESH
NX, NZ, NY = 4, 8, 8
T = 128
ORDER = (4, 5, 2, 3, 0, 1)
CHUNKS = len(ORDER)
ACROSS = (((0,), (0,)), ((), ()))


def place(y, x, z, k):
    return (y, x * 4 + z % 4, (z // 4) * 2 + k)


def remote(src, dst, send, recv, device):
    return pltpu.make_async_remote_copy(
        src_ref=src, dst_ref=dst, send_sem=send, recv_sem=recv, device_id=device, device_id_type=MESH
    )


def arrived(ref, sem):
    pltpu.make_async_copy(ref, ref, sem).wait()


def split(v):
    high = v.astype(jnp.bfloat16)
    return high, (v - high.astype(jnp.float32)).astype(jnp.bfloat16)


def across(a, parts):
    high, low = parts
    return lax.dot_general(a, high, ACROSS, preferred_element_type=jnp.float32) + lax.dot_general(
        a, low, ACROSS, preferred_element_type=jnp.float32
    )


def kernel(
    w, m, inv, sig, out, marg,
    sg, q, f, wp, pr, sb, zb, ma,
    d0, d1, d2, dr0, dr1, dr2, e0, e1, e2, yr0, yr1, yr2, xs0, xs1, xs2, zs0, zs1, zs2, g0, g1, g2,
    ssig, s1, r1, s2, r2, s3, r3, s4, r4, s5, r5, s6, r6, sm, rm,
    sd, rd, sy, ry, sx, rx, sz, rz, sg2, rg2, sc, rc,
):
    d, dr, e, yr = (d0, d1, d2), (dr0, dr1, dr2), (e0, e1, e2), (yr0, yr1, yr2)
    xs, zs, g = (xs0, xs1, xs2), (zs0, zs1, zs2), (g0, g1, g2)
    y = lax.axis_index("hyp")
    prow = lax.axis_index("prow")
    pcol = lax.axis_index("pcol")
    x, zl = prow // 4, prow % 4
    zh, k = pcol // 2, pcol % 2
    z = zh * 4 + zl
    slot = zl * 4 + zh * 2
    right, left = (x + 1) % NX, (x + 3) % NX
    partner, opposite = place(y, x, z, 1 - k), place(y, x, (z + 4) % NZ, k)

    barrier = pltpu.get_barrier_semaphore()
    greet = [partner]
    greet += [place(y, (x + a) % NX, z, c) for a in range(1, NX) for c in range(2)]
    greet += [place(y, x, (z + a) % NZ, k) for a in range(1, NZ)]
    greet += [place((y + a) % NY, x, z, k) for a in range(1, NY)]
    for who in greet:
        pl.semaphore_signal(barrier, inc=1, device_id=who, device_id_type=MESH)
    sigma_copy = pltpu.make_async_copy(sig, sg, ssig)
    sigma_copy.start()
    pl.semaphore_wait(barrier, len(greet))

    sends = []

    def go(copy):
        copy.start()
        sends.append(copy)

    kd = x % 2
    half = x // 2

    def quarter(c, at):
        return m.at[c, pl.ds(pl.multiple_of(at * 32, 32), 32)]

    for c in ORDER:

        @pl.when(kd == k)
        def _():
            pltpu.make_async_copy(quarter(c, x), q.at[c, half, k], r1.at[c]).start()

        @pl.when(kd != k)
        def _():
            remote(quarter(c, x), q.at[c, half, k], s1.at[c, 0], r1.at[c], partner).start()

        for a in range(1, NX):
            xt = (x + a) % NX
            go(remote(quarter(c, xt), q.at[c, half, k], s1.at[c, a], r1.at[c], place(y, xt, z, kd)))

    weight = w[...]
    for j in range(3):
        for s in range(2):
            for i in range(j + 1):
                d[j][s, i * T:(i + 1) * T] = weight * lax.dot_general(
                    inv[s, :, i * T:(i + 1) * T], inv[s, :, j * T:(j + 1) * T],
                    ACROSS, preferred_element_type=jnp.float32,
                )

    for c in ORDER:
        arrived(q.at[c], r1.at[c])
        for n, a in enumerate((4, 3, 5, 2, 6, 1, 7)):
            zt = (z + a) % NZ
            go(remote(q.at[c, zt // 4], f.at[c, pl.ds(slot, 2), x], s2.at[c, n], r2.at[c], place(y, x, zt, k)))
        pltpu.make_async_copy(q.at[c, zh], f.at[c, pl.ds(slot, 2), x], r2.at[c]).start()
    go(remote(m.at[0:2], ma, sm, rm, opposite))

    to_right, to_left = place(y, right, z, k), place(y, left, z, k)

    def ring_own(c):
        arrived(f.at[c, :, x], r2.at[c])
        lo, hi = f.at[c, 0:8, x], f.at[c, 8:16, x]
        go(remote(lo, lo, s3.at[c, 0], r3.at[c, 0], to_right))
        go(remote(hi, hi, s3.at[c, 1], r3.at[c, 1], to_left))
        go(remote(hi, hi, s3.at[c, 2], r3.at[c, 2], to_right))
        go(remote(lo, lo, s3.at[c, 3], r3.at[c, 3], to_left))

    def ring_relay(c):
        lo, hi = f.at[c, 0:8, left], f.at[c, 8:16, right]
        arrived(lo, r3.at[c, 0])
        go(remote(lo, lo, s4.at[c, 0], r4.at[c, 0], to_right))
        arrived(hi, r3.at[c, 1])
        go(remote(hi, hi, s4.at[c, 1], r4.at[c, 1], to_left))

    def multiply(c):
        far = (x + 2) % NX
        arrived(f.at[c, 8:16, left], r3.at[c, 2])
        arrived(f.at[c, 0:8, right], r3.at[c, 3])
        arrived(f.at[c, 0:8, far], r4.at[c, 0])
        arrived(f.at[c, 8:16, far], r4.at[c, 1])
        product = jnp.dot(sg[...], f[c].reshape(2048, T), preferred_element_type=jnp.float32)
        wp[c] = product.reshape(2, 2, T, T)
        go(remote(wp.at[c, :, 1 - k], pr.at[c], s5.at[c], r5.at[c], partner))

    def cross(c):
        arrived(pr.at[c], r5.at[c])
        theirs = wp[c, 1 - zh, k] + pr[c, 1 - zh]
        sb[c] = theirs
        go(remote(sb.at[c], zb.at[c], s6.at[c], r6.at[c], opposite))
        if c < 2:
            mine = wp[c, zh, k] + pr[c, zh]
            d[0][c] = d[0][c] + weight * (across(m[c], split(mine)) + across(ma[c], split(theirs)))

    def finish(c):
        arrived(zb.at[c], r6.at[c])
        parts = split((wp[c, zh, k] + pr[c, zh]) + zb[c])
        out[c] = -parts[0]
        j, s = divmod(c, 2)
        for i in range(j + 1 if j > 0 else 0):
            rows = pl.ds(i * T, T)
            d[j][s, rows] = d[j][s, rows] + weight * across(m[2 * i + s], parts)

    def sum_core(j):
        go(remote(d[j].at[1 - k], dr[j], sd.at[j], rd.at[j], partner))

    def sum_y(j):
        arrived(dr[j], rd.at[j])
        e[j][...] = (d[j][k] + dr[j][...]).reshape(e[j].shape)
        for n, a in enumerate((4, 3, 5, 2, 6, 1, 7)):
            yt = (y + a) % NY
            go(remote(e[j].at[yt], yr[j].at[n], sy.at[j, n], ry.at[j], place(yt, x, z, k)))

    def sum_x(j):
        arrived(yr[j], ry.at[j])
        total = e[j][y]
        for n in range(NY - 1):
            total = total + yr[j][n]
        xs[j][x] = total
        for n, a in enumerate((2, 1, 3)):
            own = xs[j].at[x]
            go(remote(own, own, sx.at[j, n], rx.at[j], place(y, (x + a) % NX, z, k)))

    def sum_z(j):
        arrived(xs[j].at[0:NX - 1], rx.at[j])
        zs[j][z] = (xs[j][0] + xs[j][1]) + (xs[j][2] + xs[j][3])
        for n, a in enumerate((4, 3, 5, 2, 6, 1, 7)):
            own = zs[j].at[z]
            go(remote(own, own, sz.at[j, n], rz.at[j], place(y, x, (z + a) % NZ, k)))

    def spread_y(j):
        arrived(zs[j].at[0:NZ - 1], rz.at[j])
        total = zs[j][0]
        for n in range(1, NZ):
            total = total + zs[j][n]
        g[j][k, y] = total
        for n, a in enumerate((4, 3, 5, 2, 6, 1, 7)):
            own = g[j].at[k, y]
            go(remote(own, own, sg2.at[j, n], rg2.at[j], place((y + a) % NY, x, z, k)))

    def spread_core(j):
        arrived(g[j].at[0, 0:NY - 1], rg2.at[j])
        go(remote(g[j].at[k], g[j].at[k], sc.at[j], rc.at[j], partner))

    def write(j):
        arrived(g[j].at[0], rc.at[j])
        for s in range(2):
            tiles = g[j][s].reshape(j + 1, T, T)
            for i in range(j + 1):
                marg[s, i * T:(i + 1) * T, j * T:(j + 1) * T] = tiles[i]
                if i != j:
                    marg[s, j * T:(j + 1) * T, i * T:(i + 1) * T] = tiles[i].T

    for t in range(CHUNKS):
        ring_own(ORDER[t])
        if t >= 1:
            ring_relay(ORDER[t - 1])
        if t == 2:
            sigma_copy.wait()
        if t >= 2:
            multiply(ORDER[t - 2])
        if t >= 3:
            cross(ORDER[t - 3])
        if t >= 4:
            finish(ORDER[t - 4])
    sum_core(2)
    ring_relay(ORDER[5])
    multiply(ORDER[4])
    sum_y(2)
    cross(ORDER[3])
    finish(ORDER[2])
    multiply(ORDER[5])
    arrived(ma, rm)
    cross(ORDER[4])
    cross(ORDER[5])
    sum_core(0)
    finish(ORDER[3])
    sum_core(1)
    sum_x(2)
    sum_y(0)
    sum_y(1)
    sum_z(2)
    sum_x(0)
    sum_x(1)
    spread_y(2)
    sum_z(0)
    sum_z(1)
    finish(ORDER[4])
    finish(ORDER[5])
    spread_core(2)
    spread_y(0)
    spread_y(1)
    write(2)
    spread_core(0)
    spread_core(1)
    write(0)
    write(1)

    for copy in sends:
        copy.wait_send()
    for c in ORDER:

        @pl.when(kd != k)
        def _():
            remote(quarter(c, x), q.at[c, half, k], s1.at[c, 0], r1.at[c], partner).wait_send()


def on_device(sigma_rows, panel, live_block_rows, inv_diag, quad_weight):
    offsets = lax.broadcasted_iota(jnp.int32, (128, 2, 384), 0)
    active = offsets < live_block_rows[:, 0][None, :, None]
    masked = jnp.where(active, panel[0], jnp.zeros_like(panel[0])).reshape(128, 2, 3, T)
    masked = jnp.transpose(masked, (2, 1, 0, 3)).reshape(CHUNKS, T, T)
    inv = jnp.pad(inv_diag[0], ((0, 0), (0, 10), (0, 0)))
    weight = jnp.broadcast_to(quad_weight[:, None], (1, 128))
    f32, bf16 = jnp.float32, jnp.bfloat16
    dma = pltpu.SemaphoreType.DMA
    vmem = pl.BlockSpec(memory_space=pltpu.VMEM)
    rows = [(j + 1) * T for j in range(3)]
    negated, marginal = pl.pallas_call(
        kernel,
        out_shape=(
            jax.ShapeDtypeStruct((CHUNKS, T, T), bf16),
            jax.ShapeDtypeStruct((2, 384, 384), f32),
        ),
        in_specs=[vmem, vmem, vmem, pl.BlockSpec(memory_space=pl.ANY)],
        out_specs=(vmem, vmem),
        scratch_shapes=[
            pltpu.VMEM((512, 2048), bf16),
            pltpu.VMEM((CHUNKS, 2, 2, 32, T), bf16),
            pltpu.VMEM((CHUNKS, 16, 4, 32, T), bf16),
            pltpu.VMEM((CHUNKS, 2, 2, T, T), f32),
            pltpu.VMEM((CHUNKS, 2, T, T), f32),
            pltpu.VMEM((CHUNKS, T, T), f32),
            pltpu.VMEM((CHUNKS, T, T), f32),
            pltpu.VMEM((2, T, T), bf16),
        ]
        + [pltpu.VMEM((2, r, T), f32) for r in rows]
        + [pltpu.VMEM((r, T), f32) for r in rows]
        + [pltpu.VMEM((NY, r // NY, T), f32) for r in rows]
        + [pltpu.VMEM((NY - 1, r // NY, T), f32) for r in rows]
        + [pltpu.VMEM((NX, r // NY, T), f32) for r in rows]
        + [pltpu.VMEM((NZ, r // NY, T), f32) for r in rows]
        + [pltpu.VMEM((2, NY, r // NY, T), f32) for r in rows]
        + [
            dma,
            dma((CHUNKS, 4)), dma((CHUNKS,)),
            dma((CHUNKS, 7)), dma((CHUNKS,)),
            dma((CHUNKS, 4)), dma((CHUNKS, 4)),
            dma((CHUNKS, 2)), dma((CHUNKS, 2)),
            dma((CHUNKS,)), dma((CHUNKS,)),
            dma((CHUNKS,)), dma((CHUNKS,)),
            dma, dma,
            dma((3,)), dma((3,)),
            dma((3, 7)), dma((3,)),
            dma((3, 3)), dma((3,)),
            dma((3, 7)), dma((3,)),
            dma((3, 7)), dma((3,)),
            dma((3,)), dma((3,)),
        ],
        compiler_params=pltpu.CompilerParams(
            collective_id=0, has_side_effects=True, vmem_limit_bytes=56 * 1024 * 1024
        ),
    )(weight, masked, inv, sigma_rows[0])
    applied = jnp.transpose(negated.reshape(3, 2, T, T), (2, 1, 0, 3)).reshape(128, 2, 384)
    sigma_panel = jnp.where(active, applied, jnp.zeros_like(applied))[None]
    return (sigma_panel, marginal)


def solution(mesh):
    in_specs = (
        P("hyp", "prow", "pcol"),
        P("hyp", ("prow", "pcol"), None, None),
        P(None, ("prow", "pcol")),
        P("hyp", None, ("prow", "pcol"), None),
        P("hyp"),
    )
    out_specs = (P("hyp", ("prow", "pcol"), None, None), P())
    return jax.shard_map(
        on_device, mesh=mesh, in_specs=in_specs, out_specs=out_specs, check_vma=False
    )
```

```python
import jax
import jax.numpy as jnp
from jax import lax
from jax.experimental import pallas as pl
from jax.experimental.pallas import tpu as pltpu
from jax.sharding import PartitionSpec as P

MESH = pl.DeviceIdType.MESH
NX, NZ, NY = 4, 8, 8
T = 128
ORDER = (4, 5, 2, 3, 0, 1)
CHUNKS = len(ORDER)
ACROSS = (((0,), (0,)), ((), ()))


def place(y, x, z, k):
    return (y, x * 4 + z % 4, (z // 4) * 2 + k)


def remote(src, dst, send, recv, device):
    return pltpu.make_async_remote_copy(
        src_ref=src, dst_ref=dst, send_sem=send, recv_sem=recv, device_id=device, device_id_type=MESH
    )


def arrived(ref, sem):
    pltpu.make_async_copy(ref, ref, sem).wait()


def split(v):
    high = v.astype(jnp.bfloat16)
    return high, (v - high.astype(jnp.float32)).astype(jnp.bfloat16)


def across(a, parts):
    high, low = parts
    return lax.dot_general(a, high, ACROSS, preferred_element_type=jnp.float32) + lax.dot_general(
        a, low, ACROSS, preferred_element_type=jnp.float32
    )


def kernel(
    w, live, panel, inv, sig, out, marg,
    m, iv, ob, sg, q, f, wp, pr, sb, zb, ma,
    d0, d1, d2, dr0, dr1, dr2, e0, e1, e2, yr0, yr1, yr2, xs0, xs1, xs2, zs0, zs1, zs2, g0, g1, g2,
    ssig, s1, r1, s2, r2, s3, r3, s4, r4, s5, r5, s6, r6, sm, rm,
    sd, rd, sy, ry, sx, rx, sz, rz, sg2, rg2, sc, rc,
):
    d, dr, e, yr = (d0, d1, d2), (dr0, dr1, dr2), (e0, e1, e2), (yr0, yr1, yr2)
    xs, zs, g = (xs0, xs1, xs2), (zs0, zs1, zs2), (g0, g1, g2)
    y = lax.axis_index("hyp")
    prow = lax.axis_index("prow")
    pcol = lax.axis_index("pcol")
    x, zl = prow // 4, prow % 4
    zh, k = pcol // 2, pcol % 2
    z = zh * 4 + zl
    slot = zl * 4 + zh * 2
    right, left = (x + 1) % NX, (x + 3) % NX
    partner, opposite = place(y, x, z, 1 - k), place(y, x, (z + 4) % NZ, k)

    barrier = pltpu.get_barrier_semaphore()
    greet = [partner]
    greet += [place(y, (x + a) % NX, z, c) for a in range(1, NX) for c in range(2)]
    greet += [place(y, x, (z + a) % NZ, k) for a in range(1, NZ)]
    greet += [place((y + a) % NY, x, z, k) for a in range(1, NY)]
    for who in greet:
        pl.semaphore_signal(barrier, inc=1, device_id=who, device_id_type=MESH)
    sigma_copy = pltpu.make_async_copy(sig, sg, ssig)
    sigma_copy.start()
    weight = w[0]
    rows = lax.broadcasted_iota(jnp.int32, (T, T), 0)
    active = [rows < live[s] for s in range(2)]
    for j in range(3):
        both = panel[:, :, j * T:(j + 1) * T].astype(jnp.float32)
        for s in range(2):
            m[2 * j + s] = jnp.where(active[s], both[:, s, :], 0.0).astype(jnp.bfloat16)
    pl.semaphore_wait(barrier, len(greet))

    sends = []

    def go(copy):
        copy.start()
        sends.append(copy)

    kd = x % 2
    half = x // 2

    def quarter(c, at):
        return m.at[c, pl.ds(pl.multiple_of(at * 32, 32), 32)]

    for c in ORDER:

        @pl.when(kd == k)
        def _():
            pltpu.make_async_copy(quarter(c, x), q.at[c, half, k], r1.at[c]).start()

        @pl.when(kd != k)
        def _():
            remote(quarter(c, x), q.at[c, half, k], s1.at[c, 0], r1.at[c], partner).start()

        for a in range(1, NX):
            xt = (x + a) % NX
            go(remote(quarter(c, xt), q.at[c, half, k], s1.at[c, a], r1.at[c], place(y, xt, z, kd)))

    iv[...] = jnp.zeros_like(iv)
    both = inv[...].astype(jnp.float32)
    for s in range(2):
        iv[s, 0:6] = both[:, s, :]
        own = iv[s].astype(jnp.bfloat16)
        for j in range(3):
            for i in range(j + 1):
                d[j][s, i * T:(i + 1) * T] = weight * lax.dot_general(
                    own[:, i * T:(i + 1) * T], own[:, j * T:(j + 1) * T], ACROSS, preferred_element_type=jnp.float32
                )

    for c in ORDER:
        arrived(q.at[c], r1.at[c])
        for n, a in enumerate((4, 3, 5, 2, 6, 1, 7)):
            zt = (z + a) % NZ
            go(remote(q.at[c, zt // 4], f.at[c, pl.ds(slot, 2), x], s2.at[c, n], r2.at[c], place(y, x, zt, k)))
        pltpu.make_async_copy(q.at[c, zh], f.at[c, pl.ds(slot, 2), x], r2.at[c]).start()
    go(remote(m.at[0:2], ma, sm, rm, opposite))

    to_right, to_left = place(y, right, z, k), place(y, left, z, k)

    def ring_own(c):
        arrived(f.at[c, :, x], r2.at[c])
        lo, hi = f.at[c, 0:8, x], f.at[c, 8:16, x]
        go(remote(lo, lo, s3.at[c, 0], r3.at[c, 0], to_right))
        go(remote(hi, hi, s3.at[c, 1], r3.at[c, 1], to_left))
        go(remote(hi, hi, s3.at[c, 2], r3.at[c, 2], to_right))
        go(remote(lo, lo, s3.at[c, 3], r3.at[c, 3], to_left))

    def ring_relay(c):
        lo, hi = f.at[c, 0:8, left], f.at[c, 8:16, right]
        arrived(lo, r3.at[c, 0])
        go(remote(lo, lo, s4.at[c, 0], r4.at[c, 0], to_right))
        arrived(hi, r3.at[c, 1])
        go(remote(hi, hi, s4.at[c, 1], r4.at[c, 1], to_left))

    def multiply(c):
        far = (x + 2) % NX
        arrived(f.at[c, 8:16, left], r3.at[c, 2])
        arrived(f.at[c, 0:8, right], r3.at[c, 3])
        arrived(f.at[c, 0:8, far], r4.at[c, 0])
        arrived(f.at[c, 8:16, far], r4.at[c, 1])
        product = jnp.dot(sg[...], f[c].reshape(2048, T), preferred_element_type=jnp.float32)
        wp[c] = product.reshape(2, 2, T, T)
        go(remote(wp.at[c, :, 1 - k], pr.at[c], s5.at[c], r5.at[c], partner))

    def cross(c):
        arrived(pr.at[c], r5.at[c])
        theirs = wp[c, 1 - zh, k] + pr[c, 1 - zh]
        sb[c] = theirs
        go(remote(sb.at[c], zb.at[c], s6.at[c], r6.at[c], opposite))
        if c < 2:
            mine = wp[c, zh, k] + pr[c, zh]
            d[0][c] = d[0][c] + weight * (across(m[c], split(mine)) + across(ma[c], split(theirs)))

    def finish(c):
        arrived(zb.at[c], r6.at[c])
        parts = split((wp[c, zh, k] + pr[c, zh]) + zb[c])
        j, s = divmod(c, 2)
        negated = jnp.where(active[s], -parts[0].astype(jnp.float32), 0.0)
        if s == 0:
            ob[j] = negated
        else:
            out[:, :, j * T:(j + 1) * T] = jnp.stack([ob[j], negated], axis=1).astype(jnp.bfloat16)
        for i in range(j + 1 if j > 0 else 0):
            rows = pl.ds(i * T, T)
            d[j][s, rows] = d[j][s, rows] + weight * across(m[2 * i + s], parts)

    def sum_core(j):
        go(remote(d[j].at[1 - k], dr[j], sd.at[j], rd.at[j], partner))

    def sum_y(j):
        arrived(dr[j], rd.at[j])
        e[j][...] = (d[j][k] + dr[j][...]).reshape(e[j].shape)
        for n, a in enumerate((4, 3, 5, 2, 6, 1, 7)):
            yt = (y + a) % NY
            go(remote(e[j].at[yt], yr[j].at[n], sy.at[j, n], ry.at[j], place(yt, x, z, k)))

    def sum_x(j):
        arrived(yr[j], ry.at[j])
        total = e[j][y]
        for n in range(NY - 1):
            total = total + yr[j][n]
        xs[j][x] = total
        for n, a in enumerate((2, 1, 3)):
            own = xs[j].at[x]
            go(remote(own, own, sx.at[j, n], rx.at[j], place(y, (x + a) % NX, z, k)))

    def sum_z(j):
        arrived(xs[j].at[0:NX - 1], rx.at[j])
        zs[j][z] = (xs[j][0] + xs[j][1]) + (xs[j][2] + xs[j][3])
        for n, a in enumerate((4, 3, 5, 2, 6, 1, 7)):
            own = zs[j].at[z]
            go(remote(own, own, sz.at[j, n], rz.at[j], place(y, x, (z + a) % NZ, k)))

    def spread_y(j):
        arrived(zs[j].at[0:NZ - 1], rz.at[j])
        total = zs[j][0]
        for n in range(1, NZ):
            total = total + zs[j][n]
        g[j][k, y] = total
        for n, a in enumerate((4, 3, 5, 2, 6, 1, 7)):
            own = g[j].at[k, y]
            go(remote(own, own, sg2.at[j, n], rg2.at[j], place((y + a) % NY, x, z, k)))

    def spread_core(j):
        arrived(g[j].at[0, 0:NY - 1], rg2.at[j])
        go(remote(g[j].at[k], g[j].at[k], sc.at[j], rc.at[j], partner))

    def write(j):
        arrived(g[j].at[0], rc.at[j])
        for s in range(2):
            tiles = g[j][s].reshape(j + 1, T, T)
            for i in range(j + 1):
                marg[s, i * T:(i + 1) * T, j * T:(j + 1) * T] = tiles[i]
                if i != j:
                    marg[s, j * T:(j + 1) * T, i * T:(i + 1) * T] = tiles[i].T

    for t in range(CHUNKS):
        ring_own(ORDER[t])
        if t >= 1:
            ring_relay(ORDER[t - 1])
        if t == 2:
            sigma_copy.wait()
        if t >= 2:
            multiply(ORDER[t - 2])
        if t >= 3:
            cross(ORDER[t - 3])
        if t >= 4:
            finish(ORDER[t - 4])
    sum_core(2)
    ring_relay(ORDER[5])
    multiply(ORDER[4])
    sum_y(2)
    cross(ORDER[3])
    finish(ORDER[2])
    multiply(ORDER[5])
    arrived(ma, rm)
    cross(ORDER[4])
    cross(ORDER[5])
    sum_core(0)
    finish(ORDER[3])
    sum_core(1)
    sum_x(2)
    sum_y(0)
    sum_y(1)
    sum_z(2)
    sum_x(0)
    sum_x(1)
    spread_y(2)
    sum_z(0)
    sum_z(1)
    finish(ORDER[4])
    finish(ORDER[5])
    spread_core(2)
    spread_y(0)
    spread_y(1)
    write(2)
    spread_core(0)
    spread_core(1)
    write(0)
    write(1)

    for copy in sends:
        copy.wait_send()
    for c in ORDER:

        @pl.when(kd != k)
        def _():
            remote(quarter(c, x), q.at[c, half, k], s1.at[c, 0], r1.at[c], partner).wait_send()


def on_device(sigma_rows, panel, live_block_rows, inv_diag, quad_weight):
    f32, bf16 = jnp.float32, jnp.bfloat16
    dma = pltpu.SemaphoreType.DMA
    vmem = pl.BlockSpec(memory_space=pltpu.VMEM)
    smem = pl.BlockSpec(memory_space=pltpu.SMEM)
    rows = [(j + 1) * T for j in range(3)]
    sigma_panel, marginal = pl.pallas_call(
        kernel,
        out_shape=(
            jax.ShapeDtypeStruct((T, 2, 384), bf16),
            jax.ShapeDtypeStruct((2, 384, 384), f32),
        ),
        in_specs=[smem, smem, vmem, vmem, pl.BlockSpec(memory_space=pl.ANY)],
        out_specs=(vmem, vmem),
        scratch_shapes=[
            pltpu.VMEM((CHUNKS, T, T), bf16),
            pltpu.VMEM((2, 8, 384), f32),
            pltpu.VMEM((3, T, T), f32),
            pltpu.VMEM((512, 2048), bf16),
            pltpu.VMEM((CHUNKS, 2, 2, 32, T), bf16),
            pltpu.VMEM((CHUNKS, 16, 4, 32, T), bf16),
            pltpu.VMEM((CHUNKS, 2, 2, T, T), f32),
            pltpu.VMEM((CHUNKS, 2, T, T), f32),
            pltpu.VMEM((CHUNKS, T, T), f32),
            pltpu.VMEM((CHUNKS, T, T), f32),
            pltpu.VMEM((2, T, T), bf16),
        ]
        + [pltpu.VMEM((2, r, T), f32) for r in rows]
        + [pltpu.VMEM((r, T), f32) for r in rows]
        + [pltpu.VMEM((NY, r // NY, T), f32) for r in rows]
        + [pltpu.VMEM((NY - 1, r // NY, T), f32) for r in rows]
        + [pltpu.VMEM((NX, r // NY, T), f32) for r in rows]
        + [pltpu.VMEM((NZ, r // NY, T), f32) for r in rows]
        + [pltpu.VMEM((2, NY, r // NY, T), f32) for r in rows]
        + [
            dma,
            dma((CHUNKS, 4)), dma((CHUNKS,)),
            dma((CHUNKS, 7)), dma((CHUNKS,)),
            dma((CHUNKS, 4)), dma((CHUNKS, 4)),
            dma((CHUNKS, 2)), dma((CHUNKS, 2)),
            dma((CHUNKS,)), dma((CHUNKS,)),
            dma((CHUNKS,)), dma((CHUNKS,)),
            dma, dma,
            dma((3,)), dma((3,)),
            dma((3, 7)), dma((3,)),
            dma((3, 3)), dma((3,)),
            dma((3, 7)), dma((3,)),
            dma((3, 7)), dma((3,)),
            dma((3,)), dma((3,)),
        ],
        compiler_params=pltpu.CompilerParams(
            collective_id=0, has_side_effects=True, vmem_limit_bytes=56 * 1024 * 1024
        ),
    )(quad_weight, live_block_rows[:, 0], panel[0], jnp.transpose(inv_diag[0], (1, 0, 2)), sigma_rows[0])
    return (sigma_panel[None], marginal)


def solution(mesh):
    in_specs = (
        P("hyp", "prow", "pcol"),
        P("hyp", ("prow", "pcol"), None, None),
        P(None, ("prow", "pcol")),
        P("hyp", None, ("prow", "pcol"), None),
        P("hyp"),
    )
    out_specs = (P("hyp", ("prow", "pcol"), None, None), P())
    return jax.shard_map(
        on_device, mesh=mesh, in_specs=in_specs, out_specs=out_specs, check_vma=False
    )
```

```python
import jax
import jax.numpy as jnp
from jax import lax
from jax.experimental import pallas as pl
from jax.experimental.pallas import tpu as pltpu
from jax.sharding import PartitionSpec as P

MESH = pl.DeviceIdType.MESH
NX, NZ, NY = 4, 8, 8
T = 128
ORDER = (4, 5, 2, 3, 0, 1)
CHUNKS = len(ORDER)
ACROSS = (((0,), (0,)), ((), ()))


def place(y, x, z, k):
    return (y, x * 4 + z % 4, (z // 4) * 2 + k)


def remote(src, dst, send, recv, device):
    return pltpu.make_async_remote_copy(
        src_ref=src, dst_ref=dst, send_sem=send, recv_sem=recv, device_id=device, device_id_type=MESH
    )


def arrived(ref, sem):
    pltpu.make_async_copy(ref, ref, sem).wait()


def split(v):
    high = v.astype(jnp.bfloat16)
    return high, (v - high.astype(jnp.float32)).astype(jnp.bfloat16)


def across(a, parts):
    high, low = parts
    return lax.dot_general(a, high, ACROSS, preferred_element_type=jnp.float32) + lax.dot_general(
        a, low, ACROSS, preferred_element_type=jnp.float32
    )


def kernel(
    w, live_far, panel_far, inv_far, sig, out, marg,
    live, panel, inv, lsem, m, iv, ob, sg, q, f, wp, pr, sb, zb, ma,
    d0, d1, d2, dr0, dr1, dr2, e0, e1, e2, yr0, yr1, yr2, xs0, xs1, xs2, zs0, zs1, zs2, g0, g1, g2,
    ssig, s1, r1, s2, r2, s3, r3, s4, r4, s5, r5, s6, r6, sm, rm,
    sd, rd, sy, ry, sx, rx, sz, rz, sg2, rg2, sc, rc,
):
    d, dr, e, yr = (d0, d1, d2), (dr0, dr1, dr2), (e0, e1, e2), (yr0, yr1, yr2)
    xs, zs, g = (xs0, xs1, xs2), (zs0, zs1, zs2), (g0, g1, g2)
    y = lax.axis_index("hyp")
    prow = lax.axis_index("prow")
    pcol = lax.axis_index("pcol")
    x, zl = prow // 4, prow % 4
    zh, k = pcol // 2, pcol % 2
    z = zh * 4 + zl
    slot = zl * 4 + zh * 2
    right, left = (x + 1) % NX, (x + 3) % NX
    partner, opposite = place(y, x, z, 1 - k), place(y, x, (z + 4) % NZ, k)

    near = [
        pltpu.make_async_copy(a, b, lsem.at[n])
        for n, (a, b) in enumerate(((live_far, live), (panel_far, panel), (inv_far, inv)))
    ]
    for copy in near:
        copy.start()
    barrier = pltpu.get_barrier_semaphore()
    greet = [partner]
    greet += [place(y, (x + a) % NX, z, c) for a in range(1, NX) for c in range(2)]
    greet += [place(y, x, (z + a) % NZ, k) for a in range(1, NZ)]
    greet += [place((y + a) % NY, x, z, k) for a in range(1, NY)]
    for who in greet:
        pl.semaphore_signal(barrier, inc=1, device_id=who, device_id_type=MESH)
    sigma_copy = pltpu.make_async_copy(sig, sg, ssig)
    sigma_copy.start()
    weight = w[0]
    for copy in near:
        copy.wait()
    rows = lax.broadcasted_iota(jnp.int32, (T, T), 0)
    active = [rows < live[s] for s in range(2)]
    for j in range(3):
        both = panel[:, :, j * T:(j + 1) * T].astype(jnp.float32)
        for s in range(2):
            m[2 * j + s] = jnp.where(active[s], both[:, s, :], 0.0).astype(jnp.bfloat16)
    pl.semaphore_wait(barrier, len(greet))

    sends = []

    def go(copy):
        copy.start()
        sends.append(copy)

    kd = x % 2
    half = x // 2

    def quarter(c, at):
        return m.at[c, pl.ds(pl.multiple_of(at * 32, 32), 32)]

    for c in ORDER:

        @pl.when(kd == k)
        def _():
            pltpu.make_async_copy(quarter(c, x), q.at[c, half, k], r1.at[c]).start()

        @pl.when(kd != k)
        def _():
            remote(quarter(c, x), q.at[c, half, k], s1.at[c, 0], r1.at[c], partner).start()

        for a in range(1, NX):
            xt = (x + a) % NX
            go(remote(quarter(c, xt), q.at[c, half, k], s1.at[c, a], r1.at[c], place(y, xt, z, kd)))

    iv[...] = jnp.zeros_like(iv)
    both = inv[...].astype(jnp.float32)
    for s in range(2):
        iv[s, 0:6] = both[:, s, :]
        own = iv[s].astype(jnp.bfloat16)
        for j in range(3):
            for i in range(j + 1):
                d[j][s, i * T:(i + 1) * T] = weight * lax.dot_general(
                    own[:, i * T:(i + 1) * T], own[:, j * T:(j + 1) * T], ACROSS, preferred_element_type=jnp.float32
                )

    for c in ORDER:
        arrived(q.at[c], r1.at[c])
        for n, a in enumerate((4, 3, 5, 2, 6, 1, 7)):
            zt = (z + a) % NZ
            go(remote(q.at[c, zt // 4], f.at[c, pl.ds(slot, 2), x], s2.at[c, n], r2.at[c], place(y, x, zt, k)))
        pltpu.make_async_copy(q.at[c, zh], f.at[c, pl.ds(slot, 2), x], r2.at[c]).start()
    go(remote(m.at[0:2], ma, sm, rm, opposite))

    to_right, to_left = place(y, right, z, k), place(y, left, z, k)

    def ring_own(c):
        arrived(f.at[c, :, x], r2.at[c])
        lo, hi = f.at[c, 0:8, x], f.at[c, 8:16, x]
        go(remote(lo, lo, s3.at[c, 0], r3.at[c, 0], to_right))
        go(remote(hi, hi, s3.at[c, 1], r3.at[c, 1], to_left))
        go(remote(hi, hi, s3.at[c, 2], r3.at[c, 2], to_right))
        go(remote(lo, lo, s3.at[c, 3], r3.at[c, 3], to_left))

    def ring_relay(c):
        lo, hi = f.at[c, 0:8, left], f.at[c, 8:16, right]
        arrived(lo, r3.at[c, 0])
        go(remote(lo, lo, s4.at[c, 0], r4.at[c, 0], to_right))
        arrived(hi, r3.at[c, 1])
        go(remote(hi, hi, s4.at[c, 1], r4.at[c, 1], to_left))

    def multiply(c):
        far = (x + 2) % NX
        arrived(f.at[c, 8:16, left], r3.at[c, 2])
        arrived(f.at[c, 0:8, right], r3.at[c, 3])
        arrived(f.at[c, 0:8, far], r4.at[c, 0])
        arrived(f.at[c, 8:16, far], r4.at[c, 1])
        product = jnp.dot(sg[...], f[c].reshape(2048, T), preferred_element_type=jnp.float32)
        wp[c] = product.reshape(2, 2, T, T)
        go(remote(wp.at[c, :, 1 - k], pr.at[c], s5.at[c], r5.at[c], partner))

    def cross(c):
        arrived(pr.at[c], r5.at[c])
        theirs = wp[c, 1 - zh, k] + pr[c, 1 - zh]
        sb[c] = theirs
        go(remote(sb.at[c], zb.at[c], s6.at[c], r6.at[c], opposite))
        if c < 2:
            mine = wp[c, zh, k] + pr[c, zh]
            d[0][c] = d[0][c] + weight * (across(m[c], split(mine)) + across(ma[c], split(theirs)))

    def finish(c):
        arrived(zb.at[c], r6.at[c])
        parts = split((wp[c, zh, k] + pr[c, zh]) + zb[c])
        j, s = divmod(c, 2)
        negated = jnp.where(active[s], -parts[0].astype(jnp.float32), 0.0)
        if s == 0:
            ob[j] = negated
        else:
            out[:, :, j * T:(j + 1) * T] = jnp.stack([ob[j], negated], axis=1).astype(jnp.bfloat16)
        for i in range(j + 1 if j > 0 else 0):
            rows = pl.ds(i * T, T)
            d[j][s, rows] = d[j][s, rows] + weight * across(m[2 * i + s], parts)

    def sum_core(j):
        go(remote(d[j].at[1 - k], dr[j], sd.at[j], rd.at[j], partner))

    def sum_y(j):
        arrived(dr[j], rd.at[j])
        e[j][...] = (d[j][k] + dr[j][...]).reshape(e[j].shape)
        for n, a in enumerate((4, 3, 5, 2, 6, 1, 7)):
            yt = (y + a) % NY
            go(remote(e[j].at[yt], yr[j].at[n], sy.at[j, n], ry.at[j], place(yt, x, z, k)))

    def sum_x(j):
        arrived(yr[j], ry.at[j])
        total = e[j][y]
        for n in range(NY - 1):
            total = total + yr[j][n]
        xs[j][x] = total
        for n, a in enumerate((2, 1, 3)):
            own = xs[j].at[x]
            go(remote(own, own, sx.at[j, n], rx.at[j], place(y, (x + a) % NX, z, k)))

    def sum_z(j):
        arrived(xs[j].at[0:NX - 1], rx.at[j])
        zs[j][z] = (xs[j][0] + xs[j][1]) + (xs[j][2] + xs[j][3])
        for n, a in enumerate((4, 3, 5, 2, 6, 1, 7)):
            own = zs[j].at[z]
            go(remote(own, own, sz.at[j, n], rz.at[j], place(y, x, (z + a) % NZ, k)))

    def spread_y(j):
        arrived(zs[j].at[0:NZ - 1], rz.at[j])
        total = zs[j][0]
        for n in range(1, NZ):
            total = total + zs[j][n]
        g[j][k, y] = total
        for n, a in enumerate((4, 3, 5, 2, 6, 1, 7)):
            own = g[j].at[k, y]
            go(remote(own, own, sg2.at[j, n], rg2.at[j], place((y + a) % NY, x, z, k)))

    def spread_core(j):
        arrived(g[j].at[0, 0:NY - 1], rg2.at[j])
        go(remote(g[j].at[k], g[j].at[k], sc.at[j], rc.at[j], partner))

    def write(j):
        arrived(g[j].at[0], rc.at[j])
        for s in range(2):
            tiles = g[j][s].reshape(j + 1, T, T)
            for i in range(j + 1):
                marg[s, i * T:(i + 1) * T, j * T:(j + 1) * T] = tiles[i]
                if i != j:
                    marg[s, j * T:(j + 1) * T, i * T:(i + 1) * T] = tiles[i].T

    for t in range(CHUNKS):
        ring_own(ORDER[t])
        if t >= 1:
            ring_relay(ORDER[t - 1])
        if t == 2:
            sigma_copy.wait()
        if t >= 2:
            multiply(ORDER[t - 2])
        if t >= 3:
            cross(ORDER[t - 3])
        if t >= 4:
            finish(ORDER[t - 4])
    sum_core(2)
    ring_relay(ORDER[5])
    multiply(ORDER[4])
    sum_y(2)
    cross(ORDER[3])
    finish(ORDER[2])
    multiply(ORDER[5])
    arrived(ma, rm)
    cross(ORDER[4])
    cross(ORDER[5])
    sum_core(0)
    finish(ORDER[3])
    sum_core(1)
    sum_x(2)
    sum_y(0)
    sum_y(1)
    sum_z(2)
    sum_x(0)
    sum_x(1)
    spread_y(2)
    sum_z(0)
    sum_z(1)
    finish(ORDER[4])
    finish(ORDER[5])
    spread_core(2)
    spread_y(0)
    spread_y(1)
    write(2)
    spread_core(0)
    spread_core(1)
    write(0)
    write(1)

    for copy in sends:
        copy.wait_send()
    for c in ORDER:

        @pl.when(kd != k)
        def _():
            remote(quarter(c, x), q.at[c, half, k], s1.at[c, 0], r1.at[c], partner).wait_send()


def on_device(sigma_rows, panel, live_block_rows, inv_diag, quad_weight):
    f32, bf16 = jnp.float32, jnp.bfloat16
    dma = pltpu.SemaphoreType.DMA
    vmem = pl.BlockSpec(memory_space=pltpu.VMEM)
    smem = pl.BlockSpec(memory_space=pltpu.SMEM)
    hbm = pl.BlockSpec(memory_space=pltpu.HBM)
    rows = [(j + 1) * T for j in range(3)]
    sigma_panel, marginal = pl.pallas_call(
        kernel,
        out_shape=(
            jax.ShapeDtypeStruct((T, 2, 384), bf16),
            jax.ShapeDtypeStruct((2, 384, 384), f32),
        ),
        in_specs=[smem, hbm, hbm, hbm, hbm],
        out_specs=(vmem, vmem),
        scratch_shapes=[
            pltpu.SMEM((2,), jnp.int32),
            pltpu.VMEM((T, 2, 384), bf16),
            pltpu.VMEM((6, 2, 384), bf16),
            dma((3,)),
            pltpu.VMEM((CHUNKS, T, T), bf16),
            pltpu.VMEM((2, 8, 384), f32),
            pltpu.VMEM((3, T, T), f32),
            pltpu.VMEM((512, 2048), bf16),
            pltpu.VMEM((CHUNKS, 2, 2, 32, T), bf16),
            pltpu.VMEM((CHUNKS, 16, 4, 32, T), bf16),
            pltpu.VMEM((CHUNKS, 2, 2, T, T), f32),
            pltpu.VMEM((CHUNKS, 2, T, T), f32),
            pltpu.VMEM((CHUNKS, T, T), f32),
            pltpu.VMEM((CHUNKS, T, T), f32),
            pltpu.VMEM((2, T, T), bf16),
        ]
        + [pltpu.VMEM((2, r, T), f32) for r in rows]
        + [pltpu.VMEM((r, T), f32) for r in rows]
        + [pltpu.VMEM((NY, r // NY, T), f32) for r in rows]
        + [pltpu.VMEM((NY - 1, r // NY, T), f32) for r in rows]
        + [pltpu.VMEM((NX, r // NY, T), f32) for r in rows]
        + [pltpu.VMEM((NZ, r // NY, T), f32) for r in rows]
        + [pltpu.VMEM((2, NY, r // NY, T), f32) for r in rows]
        + [
            dma,
            dma((CHUNKS, 4)), dma((CHUNKS,)),
            dma((CHUNKS, 7)), dma((CHUNKS,)),
            dma((CHUNKS, 4)), dma((CHUNKS, 4)),
            dma((CHUNKS, 2)), dma((CHUNKS, 2)),
            dma((CHUNKS,)), dma((CHUNKS,)),
            dma((CHUNKS,)), dma((CHUNKS,)),
            dma, dma,
            dma((3,)), dma((3,)),
            dma((3, 7)), dma((3,)),
            dma((3, 3)), dma((3,)),
            dma((3, 7)), dma((3,)),
            dma((3, 7)), dma((3,)),
            dma((3,)), dma((3,)),
        ],
        compiler_params=pltpu.CompilerParams(
            collective_id=0, has_side_effects=True, vmem_limit_bytes=24 * 1024 * 1024
        ),
    )(
        quad_weight,
        *(
            pltpu.with_memory_space_constraint(v, pltpu.HBM)
            for v in (live_block_rows[:, 0], panel[0], jnp.transpose(inv_diag[0], (1, 0, 2)), sigma_rows[0])
        ),
    )
    return (sigma_panel[None], marginal)


def solution(mesh):
    in_specs = (
        P("hyp", "prow", "pcol"),
        P("hyp", ("prow", "pcol"), None, None),
        P(None, ("prow", "pcol")),
        P("hyp", None, ("prow", "pcol"), None),
        P("hyp"),
    )
    out_specs = (P("hyp", ("prow", "pcol"), None, None), P())
    return jax.shard_map(
        on_device, mesh=mesh, in_specs=in_specs, out_specs=out_specs, check_vma=False
    )
```
